32 devices in a mesh: dp: 8 (over z, y), own: 4 (over x, core).
Axes of the slice: x: 2, y: 2, z: 4, core: 2. Of those that a mesh axis runs over, the one named last changes fastest.
Arguments:
- block_grads: float32 [8, 18, 768, 768], P('dp', None, 'own'), may hold values from -48 to 48
- table_grads: float32 [8, 4096, 768], P('dp', 'own'), may hold values from -48 to 48
- bias_grads: float32 [8, 11520], P('dp', 'own'), may hold values from -6 to 6
- owners: int32 [18], replicated, may hold values from 0 to 3, as said below
- step_count: int32 [1], replicated, may hold values from 1 to 29
- left_stat: float32 [20, 768, 768], P('own', 'dp'), may hold values from -1 to 6, as said below
- right_stat: float32 [20, 768, 768], P('own', 'dp'), may hold values from -1 to 6, as said below
- left_root: float32 [20, 768, 768], P('own', 'dp'), may hold values from -1 to 6, as said below
- right_root: float32 [20, 768, 768], P('own', 'dp'), may hold values from -1 to 6, as said below
- block_first: float32 [20, 768, 768], P('own', 'dp'), may hold values from -0.125 to 0.125
- block_second: float32 [20, 768, 768], P('own', 'dp'), may hold values from 0.0001 to 0.01
- block_master: float32 [20, 768, 768], P('own', 'dp'), may hold values from -0.21875 to 0.21875
- table_right: float32 [768, 768], P(('dp', 'own')), may hold values from -1 to 6, as said below
- table_root: float32 [768, 768], replicated, may hold values from -1 to 6, as said below
- table_first: float32 [4, 1024, 768], P('own', 'dp'), may hold values from -0.125 to 0.125
- table_second: float32 [4, 1024, 768], P('own', 'dp'), may hold values from 0.0001 to 0.01
- table_master: float32 [4, 1024, 768], P('own', 'dp'), may hold values from -0.21875 to 0.21875
- bias_first: float32 [4, 2880], P('own', 'dp'), may hold values from -0.125 to 0.125
- bias_second: float32 [4, 2880], P('own', 'dp'), may hold values from 0.0001 to 0.01
- bias_master: float32 [4, 2880], P('own', 'dp'), may hold values from -0.125 to 0.125
Outputs:
- left_next: float32 [20, 768, 768], P('own', 'dp')
- right_next: float32 [20, 768, 768], P('own', 'dp')
- first_next: float32 [20, 768, 768], P('own', 'dp')
- second_next: float32 [20, 768, 768], P('own', 'dp')
- master_next: float32 [20, 768, 768], P('own', 'dp')
- block_weights: bfloat16 [18, 768, 768], P(None, 'own')
- table_right_next: float32 [768, 768], P(('dp', 'own'))
- table_first_next: float32 [4, 1024, 768], P('own', 'dp')
- table_second_next: float32 [4, 1024, 768], P('own', 'dp')
- table_master_next: float32 [4, 1024, 768], P('own', 'dp')
- bias_first_next: float32 [4, 2880], P('own', 'dp')
- bias_second_next: float32 [4, 2880], P('own', 'dp')
- bias_master_next: float32 [4, 2880], P('own', 'dp')
The draws below stay inside these ranges and needn't reach their ends.
Inputs may be any that keep to these rules, and one draw needn't show every extreme that they name: No owner index names more than 5 blocks and at least at least one names exactly 5; the other owners share the remaining blocks as evenly as possible. `left_stat`: Symmetric. `right_stat`: Symmetric. `left_root`: Symmetric. `right_root`: Symmetric. `table_right`: Symmetric. `table_root`: Symmetric.
All inputs are finite; a program needn't handle non-finite values.
Results may differ from the reference program's by a relative error of at most 0.0004.
Values may be sent and summed in bfloat16 or wider, within the bound.
A program may use at most 192 MiB of HBM per device.

```python
import math
import jax
import jax.numpy as jnp
from jax import lax

D = 768
BIAS = 11520
NBLK = 18
ER = 4096
CAP = 5
SLOTS = 20
N_DP = 8
N_OWN = 4


def rough_grads(key, inner, rows, columns):
    row_key, column_key, noise_key = jax.random.split(key, 3)
    position = jnp.arange(rows, dtype=jnp.float32) / max(rows - 1, 1)
    rising = jnp.power(3.0, position - 0.5)[:, None]
    row_scale = rising * jnp.power(10.0, jax.random.uniform(row_key, inner + (rows, 1)) - 0.5)
    column_scale = jnp.power(10.0, jax.random.uniform(column_key, inner + (1, columns)) - 0.5)
    full_shape = (N_DP,) + inner + (rows, columns)
    noise_draw = jnp.clip(jax.random.normal(noise_key, full_shape), -4.0, 4.0)
    return noise_draw * row_scale * column_scale / math.sqrt(N_DP)


def sym_matrix(key, lead, side, lowest, highest):
    diagonal_key, noise_key = jax.random.split(key)
    diagonal = jnp.exp(jax.random.uniform(diagonal_key, lead + (side,), minval=math.log(lowest), maxval=math.log(highest)))
    noise_draw = jnp.clip(jax.random.normal(noise_key, lead + (side, side)), -4.0, 4.0)
    mixed = (noise_draw + jnp.swapaxes(noise_draw, -1, -2)) * (0.5 / math.sqrt(side))
    identity = jnp.eye(side, dtype=jnp.float32)
    return mixed + identity * diagonal[..., None]


def draw_block_grads(key, part):
    return rough_grads(jax.random.fold_in(key, 1), (NBLK,), D, D)


def draw_table_grads(key, part):
    return rough_grads(jax.random.fold_in(key, 2), (), ER, D)


def draw_owners(key, part):
    order_key, heavy_key, rest_key = jax.random.split(jax.random.fold_in(key, 3), 3)
    ordering = jax.random.permutation(order_key, NBLK).astype(jnp.int32)
    heavy_owner = jax.random.randint(heavy_key, (), 0, N_OWN).astype(jnp.int32)
    other_owners = jax.random.permutation(rest_key, N_OWN - 1).astype(jnp.int32)
    other_owners = other_owners + (other_owners >= heavy_owner).astype(jnp.int32)
    position = jnp.arange(NBLK, dtype=jnp.int32)
    spill_rank = jnp.maximum(position - CAP, 0) % (N_OWN - 1)
    chosen = jnp.where(position < CAP, heavy_owner, other_owners[spill_rank]).astype(jnp.int32)
    return jnp.zeros((NBLK,), jnp.int32).at[ordering].set(chosen)


def draw_left_stat(key, part):
    return sym_matrix(jax.random.fold_in(key, 11), (SLOTS,), D, 0.5, 5.0)


def draw_right_stat(key, part):
    return sym_matrix(jax.random.fold_in(key, 12), (SLOTS,), D, 0.5, 5.0)


def draw_left_root(key, part):
    return sym_matrix(jax.random.fold_in(key, 13), (SLOTS,), D, 0.3, 3.0)


def draw_right_root(key, part):
    return sym_matrix(jax.random.fold_in(key, 14), (SLOTS,), D, 0.3, 3.0)


def draw_table_right(key, part):
    return sym_matrix(jax.random.fold_in(key, 15), (), D, 0.5, 5.0)


def draw_table_root(key, part):
    return sym_matrix(jax.random.fold_in(key, 16), (), D, 0.3, 3.0)


def block_levels(own_key, dims, pieces, low, top_value):
    gain = 1.0
    for dim, parts in pieces:
        steps = jax.random.uniform(jax.random.fold_in(jax.random.fold_in(own_key, 6), dim), (parts,), jnp.float32, low / len(pieces), top_value / len(pieces))
        gain = gain * jnp.repeat(jnp.exp(steps), dims[dim] // parts).reshape((-1,) + (1,) * (len(dims) - 1 - dim))
    return gain


def normal_values(rng, extent, deviation, most, pieces=(), kind=jnp.bfloat16):
    entries = deviation * jax.random.normal(rng, extent, jnp.float32)
    if pieces:
        entries = entries * block_levels(rng, extent, pieces, -0.22, 0.18)
    return jnp.clip(entries, -most, most).astype(kind)


def setup_inputs(seed: int = 0) -> dict:
    arg_keys = jax.random.split(jax.random.key(seed), 21)
    return {
        "block_grads": draw_block_grads(jax.random.fold_in(arg_keys[20], 71), 0),
        "table_grads": draw_table_grads(jax.random.fold_in(arg_keys[20], 71), 0),
        "bias_grads": normal_values(arg_keys[2], (N_DP, BIAS), 1.0, 6.0, ((0, 8), (1, 4)), jnp.float32),
        "owners": draw_owners(jax.random.fold_in(arg_keys[20], 71), 0),
        "step_count": jax.random.randint(arg_keys[4], (1,), 1, 30).astype(jnp.int32),
        "left_stat": draw_left_stat(jax.random.fold_in(arg_keys[20], 71), 0),
        "right_stat": draw_right_stat(jax.random.fold_in(arg_keys[20], 71), 0),
        "left_root": draw_left_root(jax.random.fold_in(arg_keys[20], 71), 0),
        "right_root": draw_right_root(jax.random.fold_in(arg_keys[20], 71), 0),
        "block_first": normal_values(arg_keys[9], (SLOTS, D, D), 0.02, 0.125, ((0, 4), (1, 8)), jnp.float32),
        "block_second": jnp.clip(jnp.exp(math.log(0.01) - 4.6051702 * jax.random.uniform(arg_keys[10], (SLOTS, D, D), jnp.float32) ** block_levels(arg_keys[10], (SLOTS, D, D), ((0, 4), (1, 8)), -0.2, 0.2)), 0.0001, 0.01),
        "block_master": normal_values(arg_keys[11], (SLOTS, D, D), D ** -0.5, 0.21875, ((0, 4), (1, 8)), jnp.float32),
        "table_right": draw_table_right(jax.random.fold_in(arg_keys[20], 71), 0),
        "table_root": draw_table_root(jax.random.fold_in(arg_keys[20], 71), 0),
        "table_first": normal_values(arg_keys[14], (N_OWN, ER // N_OWN, D), 0.02, 0.125, ((0, 4), (1, 8)), jnp.float32),
        "table_second": jnp.clip(jnp.exp(math.log(0.01) - 4.6051702 * jax.random.uniform(arg_keys[15], (N_OWN, ER // N_OWN, D), jnp.float32) ** block_levels(arg_keys[15], (N_OWN, ER // N_OWN, D), ((0, 4), (1, 8)), -0.2, 0.2)), 0.0001, 0.01),
        "table_master": normal_values(arg_keys[16], (N_OWN, ER // N_OWN, D), D ** -0.5, 0.21875, ((0, 4), (1, 8)), jnp.float32),
        "bias_first": normal_values(arg_keys[17], (N_OWN, BIAS // N_OWN), 0.02, 0.125, ((0, 4), (1, 8)), jnp.float32),
        "bias_second": jnp.clip(jnp.exp(math.log(0.01) - 4.6051702 * jax.random.uniform(arg_keys[18], (N_OWN, BIAS // N_OWN), jnp.float32) ** block_levels(arg_keys[18], (N_OWN, BIAS // N_OWN), ((0, 4), (1, 8)), -0.2, 0.2)), 0.0001, 0.01),
        "bias_master": normal_values(arg_keys[19], (N_OWN, BIAS // N_OWN), 0.02, 0.125, ((0, 4), (1, 8)), jnp.float32),
    }


BETA_STAT = 0.9
FIRST_DECAY = 0.9
SECOND_DECAY = 0.99
LEARN_RATE = 0.1
ADAM_EPS = 1e-08
CLIP_SCALE = 0.05
HIGHEST = lax.Precision.HIGHEST

def slot_keys(owners, capacity):
    total_blocks = owners.shape[0]
    ordering = jnp.arange(total_blocks, dtype=jnp.int32)
    earlier = (owners[:, None] == owners[None, :]) & (ordering[None, :] < ordering[:, None])
    return (owners * capacity + lax.optimization_barrier(jnp.sum(earlier.astype(jnp.int32), axis=1))).astype(jnp.int32)

def adam_step(gradient, first_moment, second_moment, step_now):
    first_next = FIRST_DECAY * first_moment + (1.0 - FIRST_DECAY) * gradient
    second_next = SECOND_DECAY * second_moment + (1.0 - SECOND_DECAY) * gradient * gradient
    step_float = step_now.astype(jnp.float32)
    fix_first = 1.0 - jnp.power(jnp.float32(FIRST_DECAY), step_float)
    fix_second = 1.0 - jnp.power(jnp.float32(SECOND_DECAY), step_float)
    direction = first_next / fix_first / (jnp.sqrt(second_next / fix_second) + ADAM_EPS)
    return (first_next, second_next, direction)

def reference(block_grads, table_grads, bias_grads, owners, step_count, left_stat, right_stat, left_root, right_root, block_first, block_second, block_master, table_right, table_root, table_first, table_second, table_master, bias_first, bias_second, bias_master):
    summed = lax.optimization_barrier(jnp.sum(block_grads, axis=0))
    table_sum = lax.optimization_barrier(jnp.sum(table_grads, axis=0))
    bias_sum = lax.optimization_barrier(jnp.sum(bias_grads, axis=0))
    square_total = jnp.sum(summed * summed) + jnp.sum(table_sum * table_sum) + jnp.sum(bias_sum * bias_sum)
    limit = CLIP_SCALE * D * math.sqrt(NBLK)
    clip_factor = jnp.minimum(1.0, limit / (jnp.sqrt(square_total) + 1e-06))
    gradient = clip_factor * summed
    table_gradient = clip_factor * table_sum
    bias_gradient = clip_factor * bias_sum
    step_now = step_count[0]
    block_keys = slot_keys(owners, CAP)
    left_term = jnp.einsum('bij,bkj->bik', gradient, gradient, precision=HIGHEST)
    right_term = jnp.einsum('bji,bjk->bik', gradient, gradient, precision=HIGHEST)
    front_part = jnp.einsum('bij,bjk->bik', left_root[block_keys], gradient, precision=HIGHEST)
    shampoo = jnp.einsum('bij,bjk->bik', front_part, right_root[block_keys], precision=HIGHEST)
    first_blocks, second_blocks, adam_dir = adam_step(gradient, block_first[block_keys], block_second[block_keys], step_now)
    graft_ratio = jnp.sqrt(lax.optimization_barrier(jnp.mean(adam_dir * adam_dir, axis=(1, 2))) / (lax.optimization_barrier(jnp.mean(shampoo * shampoo, axis=(1, 2))) + 1e-06))
    master_blocks = block_master[block_keys] - LEARN_RATE * shampoo * graft_ratio[:, None, None]
    left_next = left_stat.at[block_keys].set(BETA_STAT * left_stat[block_keys] + (1.0 - BETA_STAT) * left_term)
    right_next = right_stat.at[block_keys].set(BETA_STAT * right_stat[block_keys] + (1.0 - BETA_STAT) * right_term)
    first_next = block_first.at[block_keys].set(first_blocks)
    second_next = block_second.at[block_keys].set(second_blocks)
    master_next = block_master.at[block_keys].set(master_blocks)
    block_weights = master_blocks.astype(jnp.bfloat16)
    table_stat = jnp.dot(table_gradient.T, table_gradient, precision=HIGHEST, preferred_element_type=jnp.float32)
    table_right_next = BETA_STAT * table_right + (1.0 - BETA_STAT) * table_stat
    table_dir = jnp.dot(table_gradient, table_root, precision=HIGHEST, preferred_element_type=jnp.float32)
    table_first_rows, table_second_rows, table_adam = adam_step(table_gradient, table_first.reshape(ER, D), table_second.reshape(ER, D), step_now)
    table_ratio = jnp.sqrt(jnp.mean(table_adam * table_adam) / (jnp.mean(table_dir * table_dir) + 1e-06))
    table_master_rows = table_master.reshape(ER, D) - LEARN_RATE * table_dir * table_ratio
    bias_first_flat, bias_second_flat, bias_adam = adam_step(bias_gradient, bias_first.reshape(BIAS), bias_second.reshape(BIAS), step_now)
    bias_master_flat = bias_master.reshape(BIAS) - LEARN_RATE * bias_adam
    return (left_next, right_next, first_next, second_next, master_next, block_weights, table_right_next, table_first_rows.reshape(table_first.shape), table_second_rows.reshape(table_second.shape), table_master_rows.reshape(table_master.shape), bias_first_flat.reshape(bias_first.shape), bias_second_flat.reshape(bias_second.shape), bias_master_flat.reshape(bias_master.shape))
```

```python
import math

import jax
import jax.numpy as jnp
from jax import lax
from jax.experimental import pallas as pl
from jax.experimental.pallas import tpu as pltpu
from jax.sharding import PartitionSpec as P

ER = 4096


BETA_STAT = 0.9
FIRST_DECAY = 0.9
SECOND_DECAY = 0.99
LEARN_RATE = 0.1
ADAM_EPS = 1e-08
CLIP_SCALE = 0.05
HIGHEST = lax.Precision.HIGHEST


def slot_keys(owners, capacity):
    total_blocks = owners.shape[0]
    ordering = jnp.arange(total_blocks, dtype=jnp.int32)
    earlier = (owners[:, None] == owners[None, :]) & (ordering[None, :] < ordering[:, None])
    return owners * capacity + jnp.sum(earlier.astype(jnp.int32), axis=1)


def adam_step(gradient, first_moment, second_moment, step_now):
    first_next = FIRST_DECAY * first_moment + (1.0 - FIRST_DECAY) * gradient
    second_next = SECOND_DECAY * second_moment + (1.0 - SECOND_DECAY) * gradient * gradient
    step_float = step_now.astype(jnp.float32)
    fix_first = 1.0 - jnp.power(jnp.float32(FIRST_DECAY), step_float)
    fix_second = 1.0 - jnp.power(jnp.float32(SECOND_DECAY), step_float)
    direction = first_next / fix_first / (jnp.sqrt(second_next / fix_second) + ADAM_EPS)
    return (first_next, second_next, direction)


def ring_kernel(
    picked_ref, grads_ref, small_ref, full_ref, sum_ref, block_buf, small_buf,
    block_send, block_recv, small_send, small_recv, own_send, own_recv, own_copy,
    gather_send, gather_recv,
):
    owners, steps, capacity, part_rows, _ = block_buf.shape
    half = steps // 2
    me = lax.axis_index("dp")
    own = lax.axis_index("own")
    place = me // 2 + (me % 2) * (steps - 1 - 2 * (me // 2))

    def device_at(position):
        position = (position + 2 * steps) % steps
        side = position // half
        return 2 * (position + side * (steps - 1 - 2 * position)) + side

    ahead = device_at(place + 1)
    behind = device_at(place - 1)
    barrier = pltpu.get_barrier_semaphore()
    for peer in (ahead, behind):
        pl.semaphore_signal(
            barrier, inc=1, device_id=(peer, own), device_id_type=pl.DeviceIdType.MESH
        )
    for shift in range(1, owners):
        pl.semaphore_signal(
            barrier,
            inc=1,
            device_id=(me, (own + shift) % owners),
            device_id_type=pl.DeviceIdType.MESH,
        )
    pl.semaphore_wait(barrier, owners + 1)

    def remote(source, target, send_sem, recv_sem, device):
        return pltpu.make_async_remote_copy(
            src_ref=source,
            dst_ref=target,
            send_sem=send_sem,
            recv_sem=recv_sem,
            device_id=device,
            device_id_type=pl.DeviceIdType.MESH,
        )

    small_rows = small_buf.shape[2]
    streams = owners + 2
    started = []

    def scatter_copy(stream, step):
        peer = (ahead if stream % 2 == 0 else behind, own)
        if stream < owners:
            return remote(
                block_buf.at[stream, step],
                block_buf.at[stream, step + 1],
                block_send.at[stream, step],
                block_recv.at[stream, step],
                peer,
            )
        lane = stream - owners
        return remote(
            small_buf.at[lane, step],
            small_buf.at[lane, step + 1],
            small_send.at[lane, step],
            small_recv.at[lane, step],
            peer,
        )

    def add_local(stream, step):
        chunk = device_at(place - 1 - step if stream % 2 == 0 else place + 1 + step)
        if stream < owners:
            first_row = pl.multiple_of(chunk * part_rows, 8)
            for slot in range(capacity):
                index = picked_ref[stream * capacity + slot]
                value = grads_ref[index, pl.ds(first_row, part_rows), :]
                if step > 0:
                    value = block_buf[stream, step, slot] + value
                block_buf[stream, step, slot] = value
        else:
            lane = stream - owners
            value = small_ref[chunk, lane * small_rows : (lane + 1) * small_rows, :]
            if step > 0:
                value = small_buf[lane, step] + value
            small_buf[lane, step] = value

    flight = {}
    for stream in range(streams):
        add_local(stream, 0)
        flight[stream] = scatter_copy(stream, 0)
        flight[stream].start()
        started.append(flight[stream])
    for step in range(1, steps):
        for stream in range(streams):
            flight[stream].wait_recv()
            add_local(stream, step)
            if step < steps - 1:
                flight[stream] = scatter_copy(stream, step)
                flight[stream].start()
                started.append(flight[stream])
    last = steps - 1
    keep = pltpu.make_async_copy(block_buf.at[own, last], full_ref.at[:, own, me], own_copy)
    keep.start()
    exchanges = []
    for shift in range(1, owners):
        target = (own + shift) % owners
        copy = remote(
            block_buf.at[target, last],
            full_ref.at[:, own, me],
            own_send.at[shift],
            own_recv.at[shift],
            (me, target),
        )
        copy.start()
        exchanges.append(copy)
        started.append(copy)
    sum_ref[:small_rows, :] = small_buf[0, last]
    sum_ref[small_rows:, :] = small_buf[1, last]
    keep.wait()
    for copy in exchanges:
        copy.wait_recv()

    def gather_copy(quarter, step):
        forward = quarter % 2 == 0
        chunk = device_at(place - step if forward else place + step)
        return remote(
            full_ref.at[:, quarter, chunk],
            full_ref.at[:, quarter, chunk],
            gather_send.at[quarter, step],
            gather_recv.at[quarter, step],
            (ahead if forward else behind, own),
        )

    for step in range(steps - 1):
        for quarter in range(owners):
            if step > 0:
                flight[quarter].wait_recv()
            flight[quarter] = gather_copy(quarter, step)
            flight[quarter].start()
            started.append(flight[quarter])
    for quarter in range(owners):
        flight[quarter].wait_recv()
    for copy in started:
        copy.wait_send()


def ring_exchange(picked, grads, small, owners, capacity):
    steps, small_rows, width = small.shape
    part_rows = grads.shape[1] // steps
    in_vmem = pl.BlockSpec(memory_space=pltpu.VMEM)
    dma = pltpu.SemaphoreType.DMA
    return pl.pallas_call(
        ring_kernel,
        out_shape=(
            jax.ShapeDtypeStruct((capacity, owners, steps, part_rows, width), jnp.float32),
            jax.ShapeDtypeStruct((small_rows, width), jnp.float32),
        ),
        in_specs=[pl.BlockSpec(memory_space=pltpu.SMEM), in_vmem, in_vmem],
        out_specs=(in_vmem, in_vmem),
        scratch_shapes=[
            pltpu.VMEM((owners, steps, capacity, part_rows, width), jnp.float32),
            pltpu.VMEM((2, steps, small_rows // 2, width), jnp.float32),
            dma((owners, steps)),
            dma((owners, steps)),
            dma((2, steps)),
            dma((2, steps)),
            dma((owners,)),
            dma((owners,)),
            dma,
            dma((owners, steps)),
            dma((owners, steps)),
        ],
        compiler_params=pltpu.CompilerParams(
            collective_id=0, has_side_effects=True, vmem_limit_bytes=52 << 20
        ),
        cost_estimate=pl.CostEstimate(flops=0, bytes_accessed=800_000_000, transcendentals=0),
        name="ring_exchange",
    )(picked, grads, small)


def local(
    block_grads,
    table_grads,
    bias_grads,
    owners,
    step_count,
    left_stat,
    right_stat,
    left_root,
    right_root,
    block_first,
    block_second,
    block_master,
    table_right,
    table_root,
    table_first,
    table_second,
    table_master,
    bias_first,
    bias_second,
    bias_master,
):
    owner_count = lax.axis_size("own")
    my_owner = lax.axis_index("own")
    my_replica = lax.axis_index("dp")
    capacity, share_rows, model_width = left_stat.shape
    blocks = owners.shape[0]
    step_now = step_count[0]
    block_keys = slot_keys(owners, capacity)
    slot_grid = jnp.arange(capacity, dtype=jnp.int32)
    buffer_keys = (
        jnp.arange(owner_count, dtype=jnp.int32)[None, :] * capacity + slot_grid[:, None]
    ).reshape(-1)
    matches = (buffer_keys[:, None] == block_keys[None, :]).astype(jnp.int32)
    picked = jnp.sum(matches * jnp.arange(blocks, dtype=jnp.int32)[None, :], axis=1)
    filled = jnp.sum(matches, axis=1).astype(jnp.float32)
    my_keys = my_owner * capacity + slot_grid
    live_slots = jnp.any(my_keys[:, None] == block_keys[None, :], axis=1)
    replicas = lax.axis_size("dp")
    table_share = table_first.shape[1]
    bias_share = bias_first.shape[1]
    if replicas == 8 and owner_count % 2 == 0 and block_grads.shape[2] % (8 * replicas) == 0:
        small = jnp.concatenate(
            [
                table_grads.reshape(replicas, table_share, model_width),
                jnp.pad(
                    bias_grads.reshape(replicas, 1, bias_share),
                    ((0, 0), (0, 15), (0, model_width - bias_share)),
                ),
            ],
            axis=1,
        )
        owner_major = (
            jnp.arange(owner_count * capacity, dtype=jnp.int32)[:, None] == block_keys[None, :]
        ).astype(jnp.int32)
        from_block = jnp.sum(owner_major * jnp.arange(blocks, dtype=jnp.int32)[None, :], axis=1)
        full_blocks, small_sum = ring_exchange(
            from_block, block_grads[0], small, owner_count, capacity
        )
        full_blocks = full_blocks.reshape(capacity, model_width, model_width)
        table_rows = small_sum[:table_share]
        bias_part = small_sum[table_share : table_share + 1, :bias_share]
        mine = lax.dynamic_slice_in_dim(full_blocks, my_replica * share_rows, share_rows, 1)
        block_square = jnp.sum(
            jnp.where(live_slots, jnp.sum(mine * mine, axis=(1, 2)), 0.0)
        )
        partial_square = (
            block_square + jnp.sum(table_rows * table_rows) + jnp.sum(bias_part * bias_part)
        )
    else:
        local_rows = block_grads[0]
        summed_rows = lax.psum(local_rows, "dp")
        block_square = jnp.where(my_replica == 0, jnp.sum(summed_rows * summed_rows), 0.0)
        chosen = jnp.take(summed_rows, picked, axis=0) * filled[:, None, None]
        arrived = lax.all_to_all(
            chosen.reshape(capacity, owner_count, summed_rows.shape[1], model_width),
            "own",
            split_axis=1,
            concat_axis=1,
            tiled=True,
        )
        full_blocks = arrived.reshape(capacity, model_width, model_width)
        table_part, bias_part = (
            lax.psum_scatter(table_grads, "dp", scatter_dimension=1, tiled=True),
            lax.psum_scatter(bias_grads, "dp", scatter_dimension=1, tiled=True),
        )
        table_rows = table_part[0]
        partial_square = (
            block_square + jnp.sum(table_rows * table_rows) + jnp.sum(bias_part * bias_part)
        )
    limit = CLIP_SCALE * model_width * math.sqrt(blocks)
    row_part = lax.dynamic_slice_in_dim(full_blocks, my_replica * share_rows, share_rows, 1)
    column_part = lax.dynamic_slice_in_dim(full_blocks, my_replica * share_rows, share_rows, 2)
    left_term = jnp.einsum("sij,skj->sik", row_part, full_blocks, precision=HIGHEST)
    right_term = jnp.einsum("sji,sjk->sik", column_part, full_blocks, precision=HIGHEST)
    front_part = jnp.einsum("sij,sjk->sik", left_root, full_blocks, precision=HIGHEST)
    shampoo = jnp.einsum(
        "sij,sjk->sik",
        front_part,
        lax.all_gather(right_root, "dp", axis=1, tiled=True),
        precision=HIGHEST,
    )
    table_stat = lax.psum_scatter(
        jnp.dot(table_rows.T, table_rows, precision=HIGHEST, preferred_element_type=jnp.float32),
        ("dp", "own"),
        scatter_dimension=0,
        tiled=True,
    )
    table_dir = jnp.dot(
        table_rows, table_root, precision=HIGHEST, preferred_element_type=jnp.float32
    )
    square_total = lax.psum(partial_square, ("dp", "own"))
    clip_factor = jnp.minimum(1.0, limit / (jnp.sqrt(square_total) + 1e-06))
    scale_square = clip_factor * clip_factor
    left_term = left_term * scale_square
    right_term = right_term * scale_square
    table_stat = table_stat * scale_square
    shampoo = shampoo * clip_factor
    table_dir = table_dir * clip_factor
    gradient_rows = clip_factor * lax.dynamic_slice_in_dim(
        full_blocks, my_replica * share_rows, share_rows, 1
    )
    first_blocks, second_blocks, adam_dir = adam_step(
        gradient_rows, block_first, block_second, step_now
    )
    table_gradient = clip_factor * table_rows
    table_first_rows, table_second_rows, table_adam = adam_step(
        table_gradient, table_first[0], table_second[0], step_now
    )
    bias_first_next, bias_second_next, bias_adam = adam_step(
        clip_factor * bias_part, bias_first, bias_second, step_now
    )
    placing = (
        jnp.arange(owner_count * capacity, dtype=jnp.int32)[:, None] == my_keys[None, :]
    ).astype(jnp.float32)
    adam_square = jnp.sum(placing * jnp.sum(adam_dir * adam_dir, axis=(1, 2))[None, :], axis=1)
    shampoo_square = jnp.sum(placing * jnp.sum(shampoo * shampoo, axis=(1, 2))[None, :], axis=1)
    graft_totals = lax.psum(
        (
            adam_square,
            shampoo_square,
            jnp.sum(table_adam * table_adam),
            jnp.sum(table_dir * table_dir),
        ),
        ("dp", "own"),
    )
    block_entries = float(model_width * model_width)
    mine_adam = lax.dynamic_slice_in_dim(graft_totals[0], my_owner * capacity, capacity, 0)
    mine_shampoo = lax.dynamic_slice_in_dim(graft_totals[1], my_owner * capacity, capacity, 0)
    graft_ratio = jnp.sqrt(mine_adam / block_entries / (mine_shampoo / block_entries + 1e-06))
    table_entries = float(ER * model_width)
    table_ratio = jnp.sqrt(
        graft_totals[2] / table_entries / (graft_totals[3] / table_entries + 1e-06)
    )
    live_mask = live_slots[:, None, None]
    left_next = jnp.where(
        live_mask, BETA_STAT * left_stat + (1.0 - BETA_STAT) * left_term, left_stat
    )
    right_next = jnp.where(
        live_mask, BETA_STAT * right_stat + (1.0 - BETA_STAT) * right_term, right_stat
    )
    first_next = jnp.where(live_mask, first_blocks, block_first)
    second_next = jnp.where(live_mask, second_blocks, block_second)
    master_next = jnp.where(
        live_mask, block_master - LEARN_RATE * shampoo * graft_ratio[:, None, None], block_master
    )
    master_low, table_stat = lax.optimization_barrier(
        (master_next.astype(jnp.bfloat16), table_stat)
    )
    whole_rows = lax.all_gather(master_low, "dp", axis=1, tiled=True)
    home_rows = lax.all_to_all(
        whole_rows.reshape(capacity, owner_count, model_width // owner_count, model_width),
        "own",
        split_axis=1,
        concat_axis=1,
        tiled=True,
    )
    back_index = block_keys % capacity * owner_count + block_keys // capacity
    block_weights = jnp.take(
        home_rows.reshape(capacity * owner_count, model_width // owner_count, model_width),
        back_index,
        axis=0,
    )
    table_right_next = BETA_STAT * table_right + (1.0 - BETA_STAT) * table_stat
    table_master_rows = table_master[0] - LEARN_RATE * table_dir * table_ratio
    bias_master_next = bias_master - LEARN_RATE * bias_adam
    return (
        left_next,
        right_next,
        first_next,
        second_next,
        master_next,
        block_weights,
        table_right_next,
        table_first_rows[None],
        table_second_rows[None],
        table_master_rows[None],
        bias_first_next,
        bias_second_next,
        bias_master_next,
    )


def solution(mesh):
    placed = (
        P("dp", None, "own", None),
        P("dp", "own", None),
        P("dp", "own"),
        P(),
        P(),
        P("own", "dp", None),
        P("own", "dp", None),
        P("own", "dp", None),
        P("own", "dp", None),
        P("own", "dp", None),
        P("own", "dp", None),
        P("own", "dp", None),
        P(("dp", "own"), None),
        P(),
        P("own", "dp", None),
        P("own", "dp", None),
        P("own", "dp", None),
        P("own", "dp"),
        P("own", "dp"),
        P("own", "dp"),
    )
    return jax.shard_map(
        local,
        mesh=mesh,
        in_specs=placed,
        out_specs=(
            P("own", "dp", None),
            P("own", "dp", None),
            P("own", "dp", None),
            P("own", "dp", None),
            P("own", "dp", None),
            P(None, "own", None),
            P(("dp", "own"), None),
            P("own", "dp", None),
            P("own", "dp", None),
            P("own", "dp", None),
            P("own", "dp"),
            P("own", "dp"),
            P("own", "dp"),
        ),
        check_vma=False,
    )
```
